32 devices in a mesh: groups: 2 (over y), pairs: 4 (over z), section: 2 (over core), sub: 2 (over x).
Axes of the slice: x: 2, y: 2, z: 4, core: 2. Of those that a mesh axis runs over, the one named last changes fastest.
Arguments:
- raw_record: bfloat16 [64, 49152], P(('groups', 'pairs', 'section'), 'sub'), parts along dimension 0, may hold values from -6 to 6
- fir_taps: float32 [64], replicated, may hold values from -0.75 to 0.75
- channel_ids: int32 [64], P('groups'), parts along dimension 0, may hold values from 0 to 31, each once
- offsets: int32 [8], P(('groups', 'sub')), parts along dimension 0, may hold values from 0 to 16324
- pair_table: int32 [32, 2], P('groups'), parts along dimension 0, may hold values from -1 to 3, as said below
Outputs:
- correlations: float32 [8, 32, 8, 2048], P(('section', 'sub'), ('groups', 'pairs')), parts along dimension 1
The draws below stay inside these ranges and needn't reach their ends.
There are 2 independent parts, one for each index of `groups`. The reference program is written for one: setup_inputs(seed, part) draws one part's arguments, and reference() takes and returns one part's arrays. A program takes and returns all parts, laid end to end along the dimension named above; an argument that names none is the same for every part. Nothing has to cross between parts.
Inputs may be any that keep to these rules, and one draw needn't show every extreme that they name: `pair_table`: each row is a pair block (I, J) with I <= J, or (-1, -1) for an empty slot. Every pair block of the 4 x 4 triangle stands in exactly one slot; all live slots of one owner share the first block I; owners p and p + 2 together hold exactly 5 pair blocks; some owner fills all 4 slots.
All inputs are finite; a program needn't handle non-finite values.
Results may differ from the reference program's by a relative error of at most 0.0075.
Values may be sent and summed in bfloat16 or wider, within the bound.
A program may use at most 128 MiB of HBM per device.

```python
import math
import jax
import jax.numpy as jnp
from jax import lax

NF = 2048
TAPS = 64
DEC = 4
BAND = 64
NSUB_DEV = 2
SPAN = 24576
NSUB = 4
CH = 32
BLK = 8
CB = 4
SLOTS = 4
N_PAIRS = 4
N_SUB = 2


def draw_pair_table(key, part):
    half_pairs = N_PAIRS // 2
    key_rows, key_flip, key_slots = jax.random.split(key, 3)
    row_pairs = jax.random.permutation(key_rows, half_pairs).astype(jnp.int32)
    flipped = jax.random.randint(key_flip, (half_pairs,), 0, 2).astype(jnp.int32)
    chip_index = jnp.arange(N_PAIRS, dtype=jnp.int32)
    column = chip_index % half_pairs
    low_row = row_pairs[column]
    is_upper = chip_index // half_pairs
    block_row = jnp.where(is_upper == flipped[column], low_row, CB - 1 - low_row)
    scores = jax.random.randint(key_slots, (N_PAIRS, SLOTS), 0, 1 << 20).astype(jnp.int32) * SLOTS + jnp.arange(SLOTS, dtype=jnp.int32)[None, :]
    entry_at_slot = jnp.argsort(scores, axis=1).astype(jnp.int32)
    live_count = CB - block_row
    live_entry = entry_at_slot < live_count[:, None]
    first_block = jnp.where(live_entry, block_row[:, None], -1)
    second_block = jnp.where(live_entry, block_row[:, None] + entry_at_slot, -1)
    return jnp.stack([first_block, second_block], axis=-1).reshape(N_PAIRS * SLOTS, 2).astype(jnp.int32)


def place_ends(values, stream_key, low, top_value):
    shape = values.shape
    place = [jax.random.randint(jax.random.fold_in(stream_key, axis), (), 0, shape[axis]) for axis in range(len(shape))]
    values = values.at[tuple(place)].set(low)
    longest = shape.index(max(shape))
    place[longest] = (place[longest] + 1) % shape[longest]
    return values.at[tuple(place)].set(top_value)


def block_levels(stream_key, shape, pieces, least, top_value):
    factor_of = 1.0
    for dim, blocks in pieces:
        steps = jax.random.uniform(jax.random.fold_in(jax.random.fold_in(stream_key, 6), dim), (blocks,), jnp.float32, least / len(pieces), top_value / len(pieces))
        factor_of = factor_of * jnp.repeat(jnp.exp(steps), shape[dim] // blocks).reshape((-1,) + (1,) * (len(shape) - 1 - dim))
    return factor_of


def centred(key, shape, deviation, reach, pieces=(), kind=jnp.bfloat16):
    level = block_levels(key, shape, pieces, -0.22, 0.18) if pieces else 1.0
    entries = jax.random.normal(key, shape, jnp.float32) * deviation * level
    return jnp.minimum(jnp.maximum(entries, -reach), reach).astype(kind)


def setup_inputs(seed: int = 0, part: int = 0) -> dict:
    arg_keys = jax.random.split(jax.random.key(seed), 6)
    part_keys = jax.random.split(jax.random.fold_in(arg_keys[5], part), 6)
    raw_record = centred(part_keys[0], (CH, N_SUB * SPAN), 1.0, 6.0, ((0, 8), (1, 2)))
    fir_taps = centred(arg_keys[1], (TAPS,), TAPS ** -0.5, 0.75, (), jnp.float32)
    channel_ids = jax.random.permutation(part_keys[2], CH).astype(jnp.int32)
    offsets = place_ends(jax.random.randint(part_keys[3], (NSUB,), 0, SPAN - DEC * (NF - 1) - TAPS + 1), jax.random.fold_in(part_keys[3], 1), 0, SPAN - DEC * (NF - 1) - TAPS).astype(jnp.int32)
    pair_table = draw_pair_table(jax.random.fold_in(jax.random.fold_in(arg_keys[5], part), 71), part)
    return {"raw_record": raw_record, "fir_taps": fir_taps, "channel_ids": channel_ids, "offsets": offsets, "pair_table": pair_table}


def forward_table(length):
    sample = jnp.arange(length, dtype=jnp.int32)[:, None]
    bin_index = jnp.arange(length // 2, dtype=jnp.int32)[None, :]
    angles = (sample * bin_index % length).astype(jnp.float32) * (2.0 * math.pi / length)
    return jnp.concatenate([jnp.cos(angles), -jnp.sin(angles)], axis=1).astype(jnp.bfloat16)

def inverse_table(length):
    bin_index = jnp.arange(length // 2, dtype=jnp.int32)[:, None]
    lag_index = jnp.arange(length, dtype=jnp.int32)[None, :]
    shifted = (lag_index + length // 2) % length
    angles = (bin_index * shifted % length).astype(jnp.float32) * (2.0 * math.pi / length)
    weight = jnp.where(bin_index == 0, 1.0, 2.0).astype(jnp.float32) / math.sqrt(length)
    return jnp.concatenate([weight * jnp.cos(angles), -weight * jnp.sin(angles)], axis=0).astype(jnp.bfloat16)

def whiten(spectrum):
    power_all = spectrum[:, :, 0] ** 2 + spectrum[:, :, 1] ** 2
    extent = power_all.shape
    banded = lax.optimization_barrier(jnp.mean(power_all.reshape(extent[0], extent[1], extent[2] // BAND, BAND), axis=-1))
    inverse_rms = jnp.repeat(lax.rsqrt(banded + 1e-06), BAND, axis=-1)
    return (spectrum * inverse_rms[:, :, None, :]).astype(jnp.bfloat16)

def reference(raw_record, fir_taps, channel_ids, offsets, pair_table):
    seg_len = DEC * (NF - 1) + TAPS
    starts = jnp.arange(NSUB, dtype=jnp.int32) // NSUB_DEV * SPAN + offsets

    def cut_window(start_at):
        return lax.dynamic_slice_in_dim(raw_record, start_at, seg_len, 1)
    windows = jax.vmap(cut_window, out_axes=1)(starts).astype(jnp.float32)
    accum = jnp.zeros((CH, NSUB, NF), jnp.float32)
    for tap_index in range(TAPS):
        accum = accum + fir_taps[tap_index] * windows[:, :, tap_index:tap_index + DEC * (NF - 1) + 1:DEC]
    decimated = accum.astype(jnp.bfloat16)
    spectrum = jnp.dot(decimated.reshape(CH * NSUB, NF), forward_table(NF), preferred_element_type=jnp.float32)
    whitened = whiten(spectrum.reshape(CH, NSUB, 2, NF // 2))
    by_channel = jnp.take(whitened, jnp.argsort(channel_ids).astype(jnp.int32), axis=0)
    lag_table = inverse_table(NF)

    def one_slot(slot_entry):
        live_slot = slot_entry[0] >= 0
        first_rows = lax.dynamic_slice_in_dim(by_channel, jnp.maximum(slot_entry[0], 0) * BLK, BLK, 0).astype(jnp.float32)
        second_rows = lax.dynamic_slice_in_dim(by_channel, jnp.maximum(slot_entry[1], 0) * BLK, BLK, 0).astype(jnp.float32)
        real_part = jnp.einsum('awk,bwk->abk', first_rows[:, :, 0], second_rows[:, :, 0]) + jnp.einsum('awk,bwk->abk', first_rows[:, :, 1], second_rows[:, :, 1])
        imag_part = jnp.einsum('awk,bwk->abk', first_rows[:, :, 1], second_rows[:, :, 0]) - jnp.einsum('awk,bwk->abk', first_rows[:, :, 0], second_rows[:, :, 1])
        cross_bins = jnp.stack([real_part, imag_part], axis=2) / NSUB
        cross_bins = jnp.where(live_slot, cross_bins, 0.0).astype(jnp.bfloat16)
        return jnp.dot(cross_bins.reshape(BLK * BLK, NF), lag_table, preferred_element_type=jnp.float32).reshape(BLK, BLK, NF)
    all_lags = lax.map(one_slot, pair_table)
    return jnp.transpose(all_lags, (1, 0, 2, 3))
```

```python
import functools
import math

import jax
import jax.numpy as jnp
import numpy as np
from jax import lax
from jax.experimental import pallas as pl
from jax.experimental.pallas import tpu as pltpu
from jax.sharding import PartitionSpec as P

NF = 2048
TAPS = 64
DEC = 4
BAND = 64
LANES = 128
FINE = LANES // DEC
COARSE = NF // FINE
BANDS = NF // 2 // BAND
REACH = 3
MESH = pl.DeviceIdType.MESH


def round_bf16(values):
    return np.asarray(values).astype(jnp.bfloat16)


@functools.cache
def tables():
    n2 = np.arange(COARSE)[:, None]
    k2 = np.arange(BAND)[None, :]
    angle = 2 * np.pi * (n2 * k2 % COARSE) / COARSE
    c, s = np.cos(angle), np.sin(angle)
    dft = np.concatenate([c, -s, -s, -c], axis=1)
    high = round_bf16(dft)
    low = round_bf16(dft - high.astype(np.float64))
    forward = np.concatenate([high, low], axis=0)
    n1 = np.arange(FINE)[:, None]
    turn = 2 * np.pi * (n1 * k2) / NF
    turn = np.concatenate([turn, turn], axis=1)
    twiddle = np.stack([np.cos(turn), np.sin(turn)]).astype(np.float32)
    bins = np.arange(NF // 2)[:, None]
    lag = (np.arange(NF)[None, :] + NF // 2) % NF
    theta = 2 * np.pi * (bins * lag % NF) / NF
    weight = np.where(bins == 0, 1.0, 2.0) / math.sqrt(NF)
    re = (weight * np.cos(theta)).reshape(BANDS, BAND, NF)
    im = (-weight * np.sin(theta)).reshape(BANDS, BAND, NF)
    inverse = round_bf16(np.concatenate([re, im], axis=1).reshape(NF, NF))
    return forward, twiddle, inverse


def turned(pair, index, size):
    y, ys = pair
    index = index % size
    if index == 0:
        return y, ys
    if index * 4 == size:
        return ys, -y
    c = math.cos(2 * math.pi * index / size)
    s = math.sin(2 * math.pi * index / size)
    return c * y + s * ys, c * ys - s * y


def fft(pairs):
    size = len(pairs)
    if size == 1:
        return pairs
    even, odd = fft(pairs[0::2]), fft(pairs[1::2])
    low, high = [], []
    for k in range(size // 2):
        a, b = even[k], turned(odd[k], k, size)
        low.append((a[0] + b[0], a[1] + b[1]))
        high.append((a[0] - b[0], a[1] - b[1]))
    return low + high


def kernel(sizes, raw, taps, ids, offs, table, forward, twiddle, inverse, out,
           held, rawf, tapf, zbuf, lhs, inv, inv_sem, z_send, x_send, c_send, recv):
    pairs, subs, rows, wins, slots, leads = sizes
    unit = rows * wins
    block = 2 * rows
    p = lax.axis_index("pairs")
    sec = lax.axis_index("section")
    sub = lax.axis_index("sub")

    load_inverse = pltpu.make_async_copy(inverse, inv, inv_sem)
    load_inverse.start()

    barrier = pltpu.get_barrier_semaphore()
    for d in range(1, pairs):
        pl.semaphore_signal(barrier, inc=1, device_id={"pairs": lax.rem(p + d, pairs)}, device_id_type=MESH)
    for d in range(1, subs):
        pl.semaphore_signal(barrier, inc=1, device_id={"sub": lax.rem(sub + d, subs)}, device_id_type=MESH)
    pl.semaphore_signal(barrier, inc=1, device_id={"section": 1 - sec}, device_id_type=MESH)

    chunks = raw.shape[1] // LANES
    for m in range(chunks):
        rawf[m * 8 : m * 8 + rows, :] = raw[:, m * LANES : (m + 1) * LANES].astype(jnp.float32)
    rawf[chunks * 8 :, :] = jnp.zeros((rawf.shape[0] - chunks * 8, LANES), jnp.float32)
    tapf[...] = jnp.zeros_like(tapf)
    tapf[0:1, 0:TAPS] = taps[...]

    wide = REACH * LANES
    tap_rows = jnp.broadcast_to(tapf[0:1, :], (FINE, wide))
    step = DEC * lax.broadcasted_iota(jnp.int32, (FINE, wide), 0)
    for w in range(wins):
        off = offs[w]
        first, rest = off // LANES, off % LANES
        shift = step + rest
        x = tap_rows
        for b in range((LANES + DEC * FINE - 1).bit_length()):
            x = jnp.where((shift >> b) & 1 == 1, pltpu.roll(x, 1 << b, 1), x)
        high = x.astype(jnp.bfloat16)
        low = (x - high.astype(jnp.float32)).astype(jnp.bfloat16)
        toeplitz = jnp.concatenate([high, low], axis=0)
        total = jnp.zeros((2 * FINE, rows * COARSE), jnp.float32)
        for s in range(REACH):
            seen = jnp.concatenate(
                [rawf[pl.ds((first + s) * 8 + r, COARSE, stride=8), :] for r in range(rows)], axis=0
            ).astype(jnp.bfloat16)
            total = total + lax.dot_general(
                toeplitz[:, s * LANES : (s + 1) * LANES], seen, (((1,), (1,)), ((), ())),
                preferred_element_type=jnp.float32)
        deci = (total[:FINE] + total[FINE:]).astype(jnp.bfloat16)
        for r in range(rows):
            part = deci[:, r * COARSE : (r + 1) * COARSE]
            z = jnp.dot(part, forward[:COARSE, :], preferred_element_type=jnp.float32) + jnp.dot(
                part, forward[COARSE:, :], preferred_element_type=jnp.float32)
            at = (w * rows + r) * FINE
            zbuf[0, at : at + FINE, :] = z[:, :LANES]
            zbuf[1, at : at + FINE, :] = z[:, LANES:]
    points = []
    for n in range(FINE):
        y = zbuf[0, pl.ds(n, unit, stride=FINE), :]
        ys = zbuf[1, pl.ds(n, unit, stride=FINE), :]
        c, s = twiddle[0, n : n + 1, :], twiddle[1, n : n + 1, :]
        points.append((c * y + s * ys, c * ys - s * y))
    bins = fft(points)
    mine = (p * 2 + sec) * subs + sub
    for k in range(BANDS):
        x = bins[k][0]
        power = jnp.sum(x * x, axis=1, keepdims=True) * (1.0 / BAND)
        held[mine, :, k * LANES : (k + 1) * LANES] = (x * lax.rsqrt(power + 1e-06)).astype(jnp.bfloat16)

    pl.semaphore_wait(barrier, pairs - 1 + subs - 1 + 1)

    def send(slot, send_sem, device):
        return pltpu.make_async_remote_copy(
            src_ref=held.at[slot], dst_ref=held.at[slot], send_sem=send_sem,
            recv_sem=recv.at[slot], device_id=device, device_id_type=MESH)

    copies = []
    for d in range(1, pairs):
        copies.append(send(mine, z_send.at[d], {"pairs": lax.rem(p + d, pairs)}))
        copies[-1].start()
    for dp in range(pairs):
        slot = (lax.rem(p + dp, pairs) * 2 + sec) * subs + sub
        if dp:
            send(slot, z_send.at[0], {"section": 1 - sec}).wait_recv()
        for d in range(1, subs):
            copies.append(send(slot, x_send.at[dp, d], {"sub": lax.rem(sub + d, subs)}))
            copies[-1].start()
        copies.append(send(slot, c_send.at[dp, 0], {"section": 1 - sec}))
        copies[-1].start()
    for dp in range(pairs):
        for d in range(1, subs):
            slot = (lax.rem(p + dp, pairs) * 2 + sec) * subs + lax.rem(sub + d, subs)
            send(slot, z_send.at[0], {"section": 1 - sec}).wait_recv()
            copies.append(send(slot, c_send.at[dp, d], {"section": 1 - sec}))
            copies[-1].start()

    count = pairs * block
    lead_rows = leads * subs * unit
    depth = pairs * 2 * subs * unit
    col = lax.broadcasted_iota(jnp.int32, (1, depth), 1)
    col_row = (col // (unit * subs)) * rows + col % rows
    plain = lax.broadcasted_iota(jnp.int32, (1, count), 1)
    col_id = jnp.full((1, depth), -1, jnp.int32)
    row_id = jnp.full((1, count), -1, jnp.int32)
    for i in range(count):
        col_id = jnp.where(col_row == i, ids[i], col_id)
        row_id = jnp.where(plain == i, ids[i], row_id)
    line = lax.broadcasted_iota(jnp.int32, (lead_rows, 1), 0)
    own = table[p * slots, 0]
    for s in range(1, slots):
        own = jnp.maximum(own, table[p * slots + s, 0])
    lead = own * block + (sec * subs + sub) * leads + line // (subs * unit)
    place = (line // rows) % (subs * wins)
    col_place = (col // unit) % subs * wins + (col // rows) % wins
    pick = jnp.where((lead == col_id) & (place == col_place), 1.0, 0.0).astype(jnp.bfloat16)
    entry = lax.broadcasted_iota(jnp.int32, (slots * block, 1), 0)
    want = jnp.full((slots * block, 1), -1, jnp.int32)
    for s in range(slots):
        live = jnp.where(table[p * slots + s, 0] >= 0, table[p * slots + s, 1] * block, -block)
        want = jnp.where(entry // block == s, live + entry % block, want)
    order = jnp.where(want == row_id, 1.0, 0.0).astype(jnp.bfloat16)

    for dp in range(pairs):
        for d in range(subs):
            slot = (lax.rem(p + dp, pairs) * 2 + 1 - sec) * subs + lax.rem(sub + d, subs)
            send(slot, z_send.at[0], {"section": 1 - sec}).wait_recv()
    for copy in copies:
        copy.wait_send()

    left = lax.broadcasted_iota(jnp.int32, (8, LANES), 1) < BAND
    top = lax.broadcasted_iota(jnp.int32, (8, LANES), 0) < rows
    scale = 1.0 / (wins * subs)
    width = 2 * LANES

    @pl.loop(0, NF // width)
    def _(chunk):
        base = pl.multiple_of(chunk * width, width)
        every = held[:, :, pl.ds(base, width)].astype(jnp.float32)
        flat = every.reshape(depth, width)
        heads = jnp.dot(pick, flat.astype(jnp.bfloat16), preferred_element_type=jnp.float32)
        crossed = [[[] for _ in range(2)] for _ in range(leads)]
        for h in range(2):
            lanes = slice(h * LANES, (h + 1) * LANES)
            half = heads[:, lanes]
            swap = pltpu.roll(half, BAND, 1)
            for q in range(pairs):
                for a in range(leads):
                    sums = []
                    for source in (half, swap):
                        two = []
                        for c in range(2):
                            t = None
                            for u in range(subs):
                                g = (q * 2 + c) * subs + u
                                at = (a * subs + u) * unit
                                v = flat[g * unit : (g + 1) * unit, lanes] * source[at : at + unit, :]
                                t = v if t is None else t + v
                            two.append(t + pltpu.roll(t, rows, 0))
                        sums.append(jnp.where(top, two[0], two[1]))
                    re, im = sums
                    crossed[a][h].append(
                        jnp.where(left, re + pltpu.roll(re, BAND, 1), pltpu.roll(im, BAND, 1) - im) * scale)
        for a in range(leads):
            cross = jnp.concatenate(
                [jnp.concatenate(crossed[a][h], axis=0) for h in range(2)], axis=1).astype(jnp.bfloat16)
            got = jnp.dot(order, cross, preferred_element_type=jnp.float32)
            lhs[a * slots * block : (a + 1) * slots * block, pl.ds(base, width)] = got.astype(jnp.bfloat16)

    load_inverse.wait()

    @pl.loop(0, NF // width)
    def _(chunk):
        base = pl.multiple_of(chunk * width, width)
        out[:, pl.ds(base, width)] = jnp.dot(
            lhs[...], inv[:, pl.ds(base, width)], preferred_element_type=jnp.float32)


def solution(mesh):
    pairs, subs = mesh.shape["pairs"], mesh.shape["sub"]

    def body(raw_record, fir_taps, channel_ids, offsets, pair_table):
        rows, wins = raw_record.shape[0], offsets.shape[0]
        slots = pair_table.shape[0] // pairs
        block = 2 * rows
        leads = block // (2 * subs)
        unit = rows * wins
        assert unit == 8 and block == 8 and wins == 2
        chunks = raw_record.shape[1] // LANES
        units = pairs * 2 * subs
        vmem = pl.BlockSpec(memory_space=pltpu.VMEM)
        smem = pl.BlockSpec(memory_space=pltpu.SMEM)
        forward, twiddle, inverse = tables()
        total = leads * slots * block
        result = pl.pallas_call(
            functools.partial(kernel, (pairs, subs, rows, wins, slots, leads)),
            out_shape=jax.ShapeDtypeStruct((total, NF), jnp.float32),
            in_specs=[vmem, vmem, smem, smem, smem, vmem, vmem, pl.BlockSpec(memory_space=pl.ANY)],
            out_specs=vmem,
            scratch_shapes=[
                pltpu.VMEM((units, unit, NF), jnp.bfloat16),
                pltpu.VMEM(((chunks + 8) * 8, LANES), jnp.float32),
                pltpu.VMEM((8, REACH * LANES), jnp.float32),
                pltpu.VMEM((2, unit * FINE, LANES), jnp.float32),
                pltpu.VMEM((total, NF), jnp.bfloat16),
                pltpu.VMEM((NF, NF), jnp.bfloat16),
                pltpu.SemaphoreType.DMA,
                pltpu.SemaphoreType.DMA((pairs,)),
                pltpu.SemaphoreType.DMA((pairs, subs)),
                pltpu.SemaphoreType.DMA((pairs, subs)),
                pltpu.SemaphoreType.DMA((units,)),
            ],
            compiler_params=pltpu.CompilerParams(
                collective_id=0, has_side_effects=True, vmem_limit_bytes=48 * 2**20),
        )(raw_record, fir_taps.reshape(1, TAPS), channel_ids, offsets, pair_table,
          jnp.asarray(forward), jnp.asarray(twiddle), jnp.asarray(inverse))
        return result.reshape(leads, slots, block, NF)

    return jax.shard_map(
        body,
        mesh=mesh,
        in_specs=(
            P(("groups", "pairs", "section"), "sub"),
            P(),
            P("groups"),
            P(("groups", "sub")),
            P("groups", None),
        ),
        out_specs=P(("section", "sub"), ("groups", "pairs"), None, None),
        check_vma=False,
    )
```

```python
import functools
import math

import jax
import jax.numpy as jnp
import numpy as np
from jax import lax
from jax.experimental import pallas as pl
from jax.experimental.pallas import tpu as pltpu
from jax.sharding import PartitionSpec as P

NF = 2048
TAPS = 64
DEC = 4
BAND = 64
LANES = 128
FINE = LANES // DEC
COARSE = NF // FINE
BANDS = NF // 2 // BAND
REACH = 3
MESH = pl.DeviceIdType.MESH


def round_bf16(values):
    return np.asarray(values).astype(jnp.bfloat16)


@functools.cache
def tables():
    n2 = np.arange(COARSE)[:, None]
    k2 = np.arange(BAND)[None, :]
    angle = 2 * np.pi * (n2 * k2 % COARSE) / COARSE
    c, s = np.cos(angle), np.sin(angle)
    dft = np.concatenate([c, -s, -s, -c], axis=1)
    high = round_bf16(dft)
    low = round_bf16(dft - high.astype(np.float64))
    forward = np.concatenate([high, low], axis=0)
    n1 = np.arange(FINE)[:, None]
    turn = 2 * np.pi * (n1 * k2) / NF
    turn = np.concatenate([turn, turn], axis=1)
    twiddle = np.stack([np.cos(turn), np.sin(turn)]).astype(np.float32)
    bins = np.arange(NF // 2)[:, None]
    lag = (np.arange(NF)[None, :] + NF // 2) % NF
    theta = 2 * np.pi * (bins * lag % NF) / NF
    weight = np.where(bins == 0, 1.0, 2.0) / math.sqrt(NF)
    re = (weight * np.cos(theta)).reshape(BANDS, BAND, NF)
    im = (-weight * np.sin(theta)).reshape(BANDS, BAND, NF)
    inverse = round_bf16(np.concatenate([re, im], axis=1).reshape(NF, NF))
    return forward, twiddle, inverse


def turned(pair, index, size):
    y, ys = pair
    index = index % size
    if index == 0:
        return y, ys
    if index * 4 == size:
        return ys, -y
    c = math.cos(2 * math.pi * index / size)
    s = math.sin(2 * math.pi * index / size)
    return c * y + s * ys, c * ys - s * y


def fft(pairs):
    size = len(pairs)
    if size == 1:
        return pairs
    even, odd = fft(pairs[0::2]), fft(pairs[1::2])
    low, high = [], []
    for k in range(size // 2):
        a, b = even[k], turned(odd[k], k, size)
        low.append((a[0] + b[0], a[1] + b[1]))
        high.append((a[0] - b[0], a[1] - b[1]))
    return low + high


def kernel(sizes, raw_in, taps_in, ids_in, offs_in, table_in, forward_in, twiddle_in, inverse, out,
           raw, taps, ids, offs, table, forward, twiddle, in_sems,
           held, rawf, tapf, zbuf, lhs, inv, inv_sem, z_send, x_send, c_send, recv):
    pairs, subs, rows, wins, slots, leads = sizes
    unit = rows * wins
    block = 2 * rows
    p = lax.axis_index("pairs")
    sec = lax.axis_index("section")
    sub = lax.axis_index("sub")

    barrier = pltpu.get_barrier_semaphore()
    for d in range(1, pairs):
        pl.semaphore_signal(barrier, inc=1, device_id={"pairs": lax.rem(p + d, pairs)}, device_id_type=MESH)
    for d in range(1, subs):
        pl.semaphore_signal(barrier, inc=1, device_id={"sub": lax.rem(sub + d, subs)}, device_id_type=MESH)
    pl.semaphore_signal(barrier, inc=1, device_id={"section": 1 - sec}, device_id_type=MESH)

    loads = [
        pltpu.make_async_copy(source, target, in_sems.at[i])
        for i, (source, target) in enumerate(
            ((taps_in, taps), (offs_in, offs), (raw_in, raw), (forward_in, forward),
             (twiddle_in, twiddle), (ids_in, ids), (table_in, table)))
    ]
    for load in loads:
        load.start()
    load_inverse = pltpu.make_async_copy(inverse, inv, inv_sem)
    load_inverse.start()
    tapf[...] = jnp.zeros_like(tapf)
    for load in loads:
        load.wait()

    chunks = raw.shape[1] // LANES
    for m in range(chunks):
        rawf[m * 8 : m * 8 + rows, :] = raw[:, m * LANES : (m + 1) * LANES].astype(jnp.float32)
    rawf[chunks * 8 :, :] = jnp.zeros((rawf.shape[0] - chunks * 8, LANES), jnp.float32)
    tapf[0:1, 0:TAPS] = taps[...]

    wide = REACH * LANES
    tap_rows = jnp.broadcast_to(tapf[0:1, :], (FINE, wide))
    step = DEC * lax.broadcasted_iota(jnp.int32, (FINE, wide), 0)
    for w in range(wins):
        off = offs[w]
        first, rest = off // LANES, off % LANES
        shift = step + rest
        x = tap_rows
        for b in range((LANES + DEC * FINE - 1).bit_length()):
            x = jnp.where((shift >> b) & 1 == 1, pltpu.roll(x, 1 << b, 1), x)
        high = x.astype(jnp.bfloat16)
        low = (x - high.astype(jnp.float32)).astype(jnp.bfloat16)
        toeplitz = jnp.concatenate([high, low], axis=0)
        total = jnp.zeros((2 * FINE, rows * COARSE), jnp.float32)
        for s in range(REACH):
            seen = jnp.concatenate(
                [rawf[pl.ds((first + s) * 8 + r, COARSE, stride=8), :] for r in range(rows)], axis=0
            ).astype(jnp.bfloat16)
            total = total + lax.dot_general(
                toeplitz[:, s * LANES : (s + 1) * LANES], seen, (((1,), (1,)), ((), ())),
                preferred_element_type=jnp.float32)
        deci = (total[:FINE] + total[FINE:]).astype(jnp.bfloat16)
        for r in range(rows):
            part = deci[:, r * COARSE : (r + 1) * COARSE]
            z = jnp.dot(part, forward[:COARSE, :], preferred_element_type=jnp.float32) + jnp.dot(
                part, forward[COARSE:, :], preferred_element_type=jnp.float32)
            at = (w * rows + r) * FINE
            zbuf[0, at : at + FINE, :] = z[:, :LANES]
            zbuf[1, at : at + FINE, :] = z[:, LANES:]
    points = []
    for n in range(FINE):
        y = zbuf[0, pl.ds(n, unit, stride=FINE), :]
        ys = zbuf[1, pl.ds(n, unit, stride=FINE), :]
        c, s = twiddle[0, n : n + 1, :], twiddle[1, n : n + 1, :]
        points.append((c * y + s * ys, c * ys - s * y))
    bins = fft(points)
    mine = (p * 2 + sec) * subs + sub
    for k in range(BANDS):
        x = bins[k][0]
        power = jnp.sum(x * x, axis=1, keepdims=True) * (1.0 / BAND)
        held[mine, :, k * LANES : (k + 1) * LANES] = (x * lax.rsqrt(power + 1e-06)).astype(jnp.bfloat16)

    pl.semaphore_wait(barrier, pairs - 1 + subs - 1 + 1)

    def send(slot, send_sem, device):
        return pltpu.make_async_remote_copy(
            src_ref=held.at[slot], dst_ref=held.at[slot], send_sem=send_sem,
            recv_sem=recv.at[slot], device_id=device, device_id_type=MESH)

    near = [p]
    for i in range(1, pairs):
        at = jnp.int32(0)
        for q in range(pairs):
            at = jnp.where(p == q, sorted(range(pairs), key=lambda t: (abs(t - q), t))[i], at)
        near.append(at)
    copies = []
    for d in range(pairs - 1, 0, -1):
        copies.append(send(mine, z_send.at[d], {"pairs": near[d]}))
        copies[-1].start()
    for dp in range(pairs):
        slot = (near[dp] * 2 + sec) * subs + sub
        if dp:
            send(slot, z_send.at[0], {"section": 1 - sec}).wait_recv()
        for d in range(1, subs):
            copies.append(send(slot, x_send.at[dp, d], {"sub": lax.rem(sub + d, subs)}))
            copies[-1].start()
        copies.append(send(slot, c_send.at[dp, 0], {"section": 1 - sec}))
        copies[-1].start()
    for dp in range(pairs):
        for d in range(1, subs):
            slot = (near[dp] * 2 + sec) * subs + lax.rem(sub + d, subs)
            send(slot, z_send.at[0], {"section": 1 - sec}).wait_recv()
            copies.append(send(slot, c_send.at[dp, d], {"section": 1 - sec}))
            copies[-1].start()

    count = pairs * block
    lead_rows = leads * subs * unit
    depth = pairs * 2 * subs * unit
    col = lax.broadcasted_iota(jnp.int32, (1, depth), 1)
    col_row = (col // (unit * subs)) * rows + col % rows
    plain = lax.broadcasted_iota(jnp.int32, (1, count), 1)
    col_id = jnp.full((1, depth), -1, jnp.int32)
    row_id = jnp.full((1, count), -1, jnp.int32)
    for i in range(count):
        col_id = jnp.where(col_row == i, ids[i], col_id)
        row_id = jnp.where(plain == i, ids[i], row_id)
    line = lax.broadcasted_iota(jnp.int32, (lead_rows, 1), 0)
    own = table[0, p * slots]
    for s in range(1, slots):
        own = jnp.maximum(own, table[0, p * slots + s])
    lead = own * block + (sec * subs + sub) * leads + line // (subs * unit)
    place = (line // rows) % (subs * wins)
    col_place = (col // unit) % subs * wins + (col // rows) % wins
    pick = jnp.where((lead == col_id) & (place == col_place), 1.0, 0.0).astype(jnp.bfloat16)
    entry = lax.broadcasted_iota(jnp.int32, (slots * block, 1), 0)
    want = jnp.full((slots * block, 1), -1, jnp.int32)
    for s in range(slots):
        live = jnp.where(table[0, p * slots + s] >= 0, table[1, p * slots + s] * block, -block)
        want = jnp.where(entry // block == s, live + entry % block, want)
    order = jnp.where(want == row_id, 1.0, 0.0).astype(jnp.bfloat16)

    for dp in range(pairs):
        for d in range(subs):
            slot = (lax.rem(p + dp, pairs) * 2 + 1 - sec) * subs + lax.rem(sub + d, subs)
            send(slot, z_send.at[0], {"section": 1 - sec}).wait_recv()
    for copy in copies:
        copy.wait_send()

    left = lax.broadcasted_iota(jnp.int32, (8, LANES), 1) < BAND
    top = lax.broadcasted_iota(jnp.int32, (8, LANES), 0) < rows
    scale = 1.0 / (wins * subs)
    width = 2 * LANES

    for base in range(0, NF, width):
        every = held[:, :, pl.ds(base, width)].astype(jnp.float32)
        flat = every.reshape(depth, width)
        heads = jnp.dot(pick, flat.astype(jnp.bfloat16), preferred_element_type=jnp.float32)
        crossed = [[[] for _ in range(2)] for _ in range(leads)]
        for h in range(2):
            lanes = slice(h * LANES, (h + 1) * LANES)
            half = heads[:, lanes]
            swap = pltpu.roll(half, BAND, 1)
            for q in range(pairs):
                for a in range(leads):
                    sums = []
                    for source in (half, swap):
                        two = []
                        for c in range(2):
                            t = None
                            for u in range(subs):
                                g = (q * 2 + c) * subs + u
                                at = (a * subs + u) * unit
                                v = flat[g * unit : (g + 1) * unit, lanes] * source[at : at + unit, :]
                                t = v if t is None else t + v
                            two.append(t + pltpu.roll(t, rows, 0))
                        sums.append(jnp.where(top, two[0], two[1]))
                    re, im = sums
                    crossed[a][h].append(
                        jnp.where(left, re + pltpu.roll(re, BAND, 1), pltpu.roll(im, BAND, 1) - im) * scale)
        for a in range(leads):
            cross = jnp.concatenate(
                [jnp.concatenate(crossed[a][h], axis=0) for h in range(2)], axis=1).astype(jnp.bfloat16)
            got = jnp.dot(order, cross, preferred_element_type=jnp.float32)
            lhs[a * slots * block : (a + 1) * slots * block, pl.ds(base, width)] = got.astype(jnp.bfloat16)

    load_inverse.wait()

    for base in range(0, NF, width):
        out[:, pl.ds(base, width)] = jnp.dot(
            lhs[...], inv[:, pl.ds(base, width)], preferred_element_type=jnp.float32)


def solution(mesh):
    pairs, subs = mesh.shape["pairs"], mesh.shape["sub"]

    def body(raw_record, fir_taps, channel_ids, offsets, pair_table):
        rows, wins = raw_record.shape[0], offsets.shape[0]
        slots = pair_table.shape[0] // pairs
        block = 2 * rows
        leads = block // (2 * subs)
        unit = rows * wins
        assert unit == 8 and block == 8 and wins == 2
        chunks = raw_record.shape[1] // LANES
        units = pairs * 2 * subs
        vmem = pl.BlockSpec(memory_space=pltpu.VMEM)
        hbm = pl.BlockSpec(memory_space=pltpu.HBM)
        forward, twiddle, inverse = tables()
        total = leads * slots * block
        result = pl.pallas_call(
            functools.partial(kernel, (pairs, subs, rows, wins, slots, leads)),
            out_shape=jax.ShapeDtypeStruct((total, NF), jnp.float32),
            in_specs=[hbm] * 8,
            out_specs=vmem,
            scratch_shapes=[
                pltpu.VMEM(raw_record.shape, raw_record.dtype),
                pltpu.VMEM((1, TAPS), jnp.float32),
                pltpu.SMEM(channel_ids.shape, jnp.int32),
                pltpu.SMEM(offsets.shape, jnp.int32),
                pltpu.SMEM(pair_table.shape[::-1], jnp.int32),
                pltpu.VMEM(forward.shape, jnp.bfloat16),
                pltpu.VMEM(twiddle.shape, jnp.float32),
                pltpu.SemaphoreType.DMA((7,)),
                pltpu.VMEM((units, unit, NF), jnp.bfloat16),
                pltpu.VMEM(((chunks + 8) * 8, LANES), jnp.float32),
                pltpu.VMEM((8, REACH * LANES), jnp.float32),
                pltpu.VMEM((2, unit * FINE, LANES), jnp.float32),
                pltpu.VMEM((total, NF), jnp.bfloat16),
                pltpu.VMEM((NF, NF), jnp.bfloat16),
                pltpu.SemaphoreType.DMA,
                pltpu.SemaphoreType.DMA((pairs,)),
                pltpu.SemaphoreType.DMA((pairs, subs)),
                pltpu.SemaphoreType.DMA((pairs, subs)),
                pltpu.SemaphoreType.DMA((units,)),
            ],
            compiler_params=pltpu.CompilerParams(
                collective_id=0, has_side_effects=True, vmem_limit_bytes=67043328),
        )(raw_record, fir_taps.reshape(1, TAPS), channel_ids, offsets, pair_table.T,
          jnp.asarray(forward), jnp.asarray(twiddle), jnp.asarray(inverse))
        return result.reshape(leads, slots, block, NF)

    return jax.shard_map(
        body,
        mesh=mesh,
        in_specs=(
            P(("groups", "pairs", "section"), "sub"),
            P(),
            P("groups"),
            P(("groups", "sub")),
            P("groups", None),
        ),
        out_specs=P(("section", "sub"), ("groups", "pairs"), None, None),
        check_vma=False,
    )
```

```python
import functools
import math

import jax
import jax.numpy as jnp
import numpy as np
from jax import lax
from jax.experimental import pallas as pl
from jax.experimental.pallas import tpu as pltpu
from jax.sharding import PartitionSpec as P

NF = 2048
TAPS = 64
DEC = 4
BAND = 64
LANES = 128
FINE = LANES // DEC
COARSE = NF // FINE
BANDS = NF // 2 // BAND
REACH = 3
MESH = pl.DeviceIdType.MESH


def round_bf16(values):
    return np.asarray(values).astype(jnp.bfloat16)


@functools.cache
def tables():
    n2 = np.arange(COARSE)[:, None]
    k2 = np.arange(BAND)[None, :]
    angle = 2 * np.pi * (n2 * k2 % COARSE) / COARSE
    c, s = np.cos(angle), np.sin(angle)
    dft = np.concatenate([c, -s, -s, -c], axis=1)
    high = round_bf16(dft)
    low = round_bf16(dft - high.astype(np.float64))
    forward = np.concatenate([high, low], axis=0)
    n1 = np.arange(FINE)[:, None]
    turn = 2 * np.pi * (n1 * k2) / NF
    turn = np.concatenate([turn, turn], axis=1)
    twiddle = np.stack([np.cos(turn), np.sin(turn)]).astype(np.float32)
    bins = np.arange(NF // 2)[:, None]
    lag = (np.arange(NF)[None, :] + NF // 2) % NF
    theta = 2 * np.pi * (bins * lag % NF) / NF
    weight = np.where(bins == 0, 1.0, 2.0) / math.sqrt(NF)
    re = (weight * np.cos(theta)).reshape(BANDS, BAND, NF)
    im = (-weight * np.sin(theta)).reshape(BANDS, BAND, NF)
    inverse = round_bf16(np.concatenate([re, im], axis=1).reshape(NF, NF))
    return forward, twiddle, inverse


def turned(pair, index, size):
    y, ys = pair
    index = index % size
    if index == 0:
        return y, ys
    if index * 4 == size:
        return ys, -y
    c = math.cos(2 * math.pi * index / size)
    s = math.sin(2 * math.pi * index / size)
    return c * y + s * ys, c * ys - s * y


def fft(pairs):
    size = len(pairs)
    if size == 1:
        return pairs
    even, odd = fft(pairs[0::2]), fft(pairs[1::2])
    low, high = [], []
    for k in range(size // 2):
        a, b = even[k], turned(odd[k], k, size)
        low.append((a[0] + b[0], a[1] + b[1]))
        high.append((a[0] - b[0], a[1] - b[1]))
    return low + high


def kernel(sizes, raw_in, taps_in, ids_in, offs_in, table_in, forward_in, twiddle_in, inverse, out,
           raw, taps, ids, offs, table, forward, twiddle, in_sems,
           held, rawf, tapf, zbuf, lhs, inv, inv_sem, z_send, x_send, c_send, recv):
    pairs, subs, rows, wins, slots, leads = sizes
    unit = rows * wins
    block = 2 * rows
    p = lax.axis_index("pairs")
    sec = lax.axis_index("section")
    sub = lax.axis_index("sub")

    barrier = pltpu.get_barrier_semaphore()
    for dp in range(pairs):
        for d in range(subs):
            if dp or d:
                pl.semaphore_signal(
                    barrier, inc=1, device_id_type=MESH,
                    device_id={"pairs": lax.rem(p + dp, pairs), "sub": lax.rem(sub + d, subs)})
    pl.semaphore_signal(barrier, inc=1, device_id={"section": 1 - sec}, device_id_type=MESH)

    loads = [
        pltpu.make_async_copy(source, target, in_sems.at[i])
        for i, (source, target) in enumerate(
            ((taps_in, taps), (offs_in, offs), (raw_in, raw), (forward_in, forward),
             (twiddle_in, twiddle), (ids_in, ids), (table_in, table)))
    ]
    for load in loads:
        load.start()
    load_inverse = pltpu.make_async_copy(inverse, inv, inv_sem)
    load_inverse.start()
    tapf[...] = jnp.zeros_like(tapf)
    for load in loads:
        load.wait()

    chunks = raw.shape[1] // LANES
    for m in range(chunks):
        rawf[m * 8 : m * 8 + rows, :] = raw[:, m * LANES : (m + 1) * LANES].astype(jnp.float32)
    rawf[chunks * 8 :, :] = jnp.zeros((rawf.shape[0] - chunks * 8, LANES), jnp.float32)
    tapf[0:1, 0:TAPS] = taps[...]

    wide = REACH * LANES
    tap_rows = jnp.broadcast_to(tapf[0:1, :], (FINE, wide))
    step = DEC * lax.broadcasted_iota(jnp.int32, (FINE, wide), 0)
    for w in range(wins):
        off = offs[w]
        first, rest = off // LANES, off % LANES
        shift = step + rest
        x = tap_rows
        for b in range((LANES + DEC * FINE - 1).bit_length()):
            x = jnp.where((shift >> b) & 1 == 1, pltpu.roll(x, 1 << b, 1), x)
        high = x.astype(jnp.bfloat16)
        low = (x - high.astype(jnp.float32)).astype(jnp.bfloat16)
        toeplitz = jnp.concatenate([high, low], axis=0)
        total = jnp.zeros((2 * FINE, rows * COARSE), jnp.float32)
        for s in range(REACH):
            seen = jnp.concatenate(
                [rawf[pl.ds((first + s) * 8 + r, COARSE, stride=8), :] for r in range(rows)], axis=0
            ).astype(jnp.bfloat16)
            total = total + lax.dot_general(
                toeplitz[:, s * LANES : (s + 1) * LANES], seen, (((1,), (1,)), ((), ())),
                preferred_element_type=jnp.float32)
        deci = (total[:FINE] + total[FINE:]).astype(jnp.bfloat16)
        for r in range(rows):
            part = deci[:, r * COARSE : (r + 1) * COARSE]
            z = jnp.dot(part, forward[:COARSE, :], preferred_element_type=jnp.float32) + jnp.dot(
                part, forward[COARSE:, :], preferred_element_type=jnp.float32)
            at = (w * rows + r) * FINE
            zbuf[0, at : at + FINE, :] = z[:, :LANES]
            zbuf[1, at : at + FINE, :] = z[:, LANES:]
    points = []
    for n in range(FINE):
        y = zbuf[0, pl.ds(n, unit, stride=FINE), :]
        ys = zbuf[1, pl.ds(n, unit, stride=FINE), :]
        c, s = twiddle[0, n : n + 1, :], twiddle[1, n : n + 1, :]
        points.append((c * y + s * ys, c * ys - s * y))
    bins = fft(points)
    mine = (p * 2 + sec) * subs + sub
    for k in range(BANDS):
        x = bins[k][0]
        power = jnp.sum(x * x, axis=1, keepdims=True) * (1.0 / BAND)
        held[mine, :, k * LANES : (k + 1) * LANES] = (x * lax.rsqrt(power + 1e-06)).astype(jnp.bfloat16)

    pl.semaphore_wait(barrier, pairs * subs)

    def send(slot, send_sem, device):
        return pltpu.make_async_remote_copy(
            src_ref=held.at[slot], dst_ref=held.at[slot], send_sem=send_sem,
            recv_sem=recv.at[slot], device_id=device, device_id_type=MESH)

    near = [p]
    for i in range(1, pairs):
        at = jnp.int32(0)
        for q in range(pairs):
            at = jnp.where(p == q, sorted(range(pairs), key=lambda t: (abs(t - q), t))[i], at)
        near.append(at)
    copies = []
    for dp in range(pairs - 1, -1, -1):
        for d in range(subs - 1, -1, -1):
            if not (dp or d):
                continue
            copies.append(send(mine, x_send.at[dp, d], {"pairs": near[dp], "sub": lax.rem(sub + d, subs)}))
            copies[-1].start()
    for dp in range(pairs):
        slot = (near[dp] * 2 + sec) * subs + sub
        if dp:
            send(slot, z_send.at[0], {"section": 1 - sec}).wait_recv()
        copies.append(send(slot, c_send.at[dp, 0], {"section": 1 - sec}))
        copies[-1].start()
    for dp in range(pairs):
        for d in range(1, subs):
            slot = (near[dp] * 2 + sec) * subs + lax.rem(sub + d, subs)
            send(slot, z_send.at[0], {"section": 1 - sec}).wait_recv()
            copies.append(send(slot, c_send.at[dp, d], {"section": 1 - sec}))
            copies[-1].start()

    count = pairs * block
    lead_rows = leads * subs * unit
    depth = pairs * 2 * subs * unit
    col = lax.broadcasted_iota(jnp.int32, (1, depth), 1)
    col_row = (col // (unit * subs)) * rows + col % rows
    plain = lax.broadcasted_iota(jnp.int32, (1, count), 1)
    col_id = jnp.full((1, depth), -1, jnp.int32)
    row_id = jnp.full((1, count), -1, jnp.int32)
    for i in range(count):
        col_id = jnp.where(col_row == i, ids[i], col_id)
        row_id = jnp.where(plain == i, ids[i], row_id)
    line = lax.broadcasted_iota(jnp.int32, (lead_rows, 1), 0)
    own = table[0, p * slots]
    for s in range(1, slots):
        own = jnp.maximum(own, table[0, p * slots + s])
    lead = own * block + (sec * subs + sub) * leads + line // (subs * unit)
    place = (line // rows) % (subs * wins)
    col_place = (col // unit) % subs * wins + (col // rows) % wins
    pick = jnp.where((lead == col_id) & (place == col_place), 1.0, 0.0).astype(jnp.bfloat16)
    entry = lax.broadcasted_iota(jnp.int32, (slots * block, 1), 0)
    want = jnp.full((slots * block, 1), -1, jnp.int32)
    for s in range(slots):
        live = jnp.where(table[0, p * slots + s] >= 0, table[1, p * slots + s] * block, -block)
        want = jnp.where(entry // block == s, live + entry % block, want)
    order = jnp.where(want == row_id, 1.0, 0.0).astype(jnp.bfloat16)

    for dp in range(pairs):
        for d in range(subs):
            slot = (lax.rem(p + dp, pairs) * 2 + 1 - sec) * subs + lax.rem(sub + d, subs)
            send(slot, z_send.at[0], {"section": 1 - sec}).wait_recv()
    for copy in copies:
        copy.wait_send()

    left = lax.broadcasted_iota(jnp.int32, (8, LANES), 1) < BAND
    top = lax.broadcasted_iota(jnp.int32, (8, LANES), 0) < rows
    scale = 1.0 / (wins * subs)
    width = 2 * LANES

    for base in range(0, NF, width):
        every = held[:, :, pl.ds(base, width)].astype(jnp.float32)
        flat = every.reshape(depth, width)
        heads = jnp.dot(pick, flat.astype(jnp.bfloat16), preferred_element_type=jnp.float32)
        crossed = [[[] for _ in range(2)] for _ in range(leads)]
        for h in range(2):
            lanes = slice(h * LANES, (h + 1) * LANES)
            half = heads[:, lanes]
            swap = pltpu.roll(half, BAND, 1)
            for q in range(pairs):
                for a in range(leads):
                    sums = []
                    for source in (half, swap):
                        two = []
                        for c in range(2):
                            t = None
                            for u in range(subs):
                                g = (q * 2 + c) * subs + u
                                at = (a * subs + u) * unit
                                v = flat[g * unit : (g + 1) * unit, lanes] * source[at : at + unit, :]
                                t = v if t is None else t + v
                            two.append(t + pltpu.roll(t, rows, 0))
                        sums.append(jnp.where(top, two[0], two[1]))
                    re, im = sums
                    crossed[a][h].append(
                        jnp.where(left, re + pltpu.roll(re, BAND, 1), pltpu.roll(im, BAND, 1) - im) * scale)
        for a in range(leads):
            cross = jnp.concatenate(
                [jnp.concatenate(crossed[a][h], axis=0) for h in range(2)], axis=1).astype(jnp.bfloat16)
            got = jnp.dot(order, cross, preferred_element_type=jnp.float32)
            lhs[a * slots * block : (a + 1) * slots * block, pl.ds(base, width)] = got.astype(jnp.bfloat16)

    load_inverse.wait()

    for base in range(0, NF, width):
        out[:, pl.ds(base, width)] = jnp.dot(
            lhs[...], inv[:, pl.ds(base, width)], preferred_element_type=jnp.float32)


def solution(mesh):
    pairs, subs = mesh.shape["pairs"], mesh.shape["sub"]

    def body(raw_record, fir_taps, channel_ids, offsets, pair_table):
        rows, wins = raw_record.shape[0], offsets.shape[0]
        slots = pair_table.shape[0] // pairs
        block = 2 * rows
        leads = block // (2 * subs)
        unit = rows * wins
        assert unit == 8 and block == 8 and wins == 2
        chunks = raw_record.shape[1] // LANES
        units = pairs * 2 * subs
        vmem = pl.BlockSpec(memory_space=pltpu.VMEM)
        hbm = pl.BlockSpec(memory_space=pltpu.HBM)
        forward, twiddle, inverse = tables()
        total = leads * slots * block
        result = pl.pallas_call(
            functools.partial(kernel, (pairs, subs, rows, wins, slots, leads)),
            out_shape=jax.ShapeDtypeStruct((total, NF), jnp.float32),
            in_specs=[hbm] * 8,
            out_specs=vmem,
            scratch_shapes=[
                pltpu.VMEM(raw_record.shape, raw_record.dtype),
                pltpu.VMEM((1, TAPS), jnp.float32),
                pltpu.SMEM(channel_ids.shape, jnp.int32),
                pltpu.SMEM(offsets.shape, jnp.int32),
                pltpu.SMEM(pair_table.shape[::-1], jnp.int32),
                pltpu.VMEM(forward.shape, jnp.bfloat16),
                pltpu.VMEM(twiddle.shape, jnp.float32),
                pltpu.SemaphoreType.DMA((7,)),
                pltpu.VMEM((units, unit, NF), jnp.bfloat16),
                pltpu.VMEM(((chunks + 8) * 8, LANES), jnp.float32),
                pltpu.VMEM((8, REACH * LANES), jnp.float32),
                pltpu.VMEM((2, unit * FINE, LANES), jnp.float32),
                pltpu.VMEM((total, NF), jnp.bfloat16),
                pltpu.VMEM((NF, NF), jnp.bfloat16),
                pltpu.SemaphoreType.DMA,
                pltpu.SemaphoreType.DMA((pairs,)),
                pltpu.SemaphoreType.DMA((pairs, subs)),
                pltpu.SemaphoreType.DMA((pairs, subs)),
                pltpu.SemaphoreType.DMA((units,)),
            ],
            compiler_params=pltpu.CompilerParams(
                collective_id=0, has_side_effects=True, vmem_limit_bytes=67043328),
        )(raw_record, fir_taps.reshape(1, TAPS), channel_ids, offsets, pair_table.T,
          jnp.asarray(forward), jnp.asarray(twiddle), jnp.asarray(inverse))
        return result.reshape(leads, slots, block, NF)

    return jax.shard_map(
        body,
        mesh=mesh,
        in_specs=(
            P(("groups", "pairs", "section"), "sub"),
            P(),
            P("groups"),
            P(("groups", "sub")),
            P("groups", None),
        ),
        out_specs=P(("section", "sub"), ("groups", "pairs"), None, None),
        check_vma=False,
    )
```

```python
import functools
import math

import jax
import jax.numpy as jnp
import numpy as np
from jax import lax
from jax.experimental import pallas as pl
from jax.experimental.pallas import tpu as pltpu
from jax.sharding import PartitionSpec as P

NF = 2048
TAPS = 64
DEC = 4
BAND = 64
LANES = 128
FINE = LANES // DEC
COARSE = NF // FINE
BANDS = NF // 2 // BAND
REACH = 3
MESH = pl.DeviceIdType.MESH


def round_bf16(values):
    return np.asarray(values).astype(jnp.bfloat16)


@functools.cache
def tables():
    n2 = np.arange(COARSE)[:, None]
    k2 = np.arange(BAND)[None, :]
    angle = 2 * np.pi * (n2 * k2 % COARSE) / COARSE
    c, s = np.cos(angle), np.sin(angle)
    dft = np.concatenate([c, -s, -s, -c], axis=1)
    high = round_bf16(dft)
    low = round_bf16(dft - high.astype(np.float64))
    forward = np.concatenate([high, low], axis=0)
    n1 = np.arange(FINE)[:, None]
    turn = 2 * np.pi * (n1 * k2) / NF
    turn = np.concatenate([turn, turn], axis=1)
    twiddle = np.stack([np.cos(turn), np.sin(turn)]).astype(np.float32)
    bins = np.arange(NF // 2)[:, None]
    lag = (np.arange(NF)[None, :] + NF // 2) % NF
    theta = 2 * np.pi * (bins * lag % NF) / NF
    weight = np.where(bins == 0, 1.0, 2.0) / math.sqrt(NF)
    re = (weight * np.cos(theta)).reshape(BANDS, BAND, NF)
    im = (-weight * np.sin(theta)).reshape(BANDS, BAND, NF)
    inverse = round_bf16(np.concatenate([re, im], axis=1).reshape(NF, NF))
    return forward, twiddle, inverse


def turned(pair, index, size):
    y, ys = pair
    index = index % size
    if index == 0:
        return y, ys
    if index * 4 == size:
        return ys, -y
    c = math.cos(2 * math.pi * index / size)
    s = math.sin(2 * math.pi * index / size)
    return c * y + s * ys, c * ys - s * y


def fft(pairs):
    size = len(pairs)
    if size == 1:
        return pairs
    even, odd = fft(pairs[0::2]), fft(pairs[1::2])
    low, high = [], []
    for k in range(size // 2):
        a, b = even[k], turned(odd[k], k, size)
        low.append((a[0] + b[0], a[1] + b[1]))
        high.append((a[0] - b[0], a[1] - b[1]))
    return low + high


def kernel(sizes, raw_in, taps_in, ids_in, offs_in, table_in, forward_in, twiddle_in, inverse, out,
           raw, taps, ids, offs, table, forward, twiddle, in_sems,
           held, rawf, tapf, zbuf, lhs, inv, inv_sem, z_send, x_send, c_send, recv):
    pairs, subs, rows, wins, slots, leads = sizes
    unit = rows * wins
    block = 2 * rows
    p = lax.axis_index("pairs")
    sec = lax.axis_index("section")
    sub = lax.axis_index("sub")

    barrier = pltpu.get_barrier_semaphore()
    for dp in range(pairs):
        for d in range(subs):
            if dp or d:
                pl.semaphore_signal(
                    barrier, inc=1, device_id_type=MESH,
                    device_id={"pairs": lax.rem(p + dp, pairs), "sub": lax.rem(sub + d, subs)})
    pl.semaphore_signal(barrier, inc=1, device_id={"section": 1 - sec}, device_id_type=MESH)

    loads = [
        pltpu.make_async_copy(source, target, in_sems.at[i])
        for i, (source, target) in enumerate(
            ((taps_in, taps), (offs_in, offs), (raw_in, raw), (forward_in, forward),
             (twiddle_in, twiddle), (ids_in, ids), (table_in, table)))
    ]
    for load in loads:
        load.start()
    load_inverse = pltpu.make_async_copy(inverse, inv, inv_sem)
    load_inverse.start()
    tapf[...] = jnp.zeros_like(tapf)
    for load in loads:
        load.wait()

    chunks = raw.shape[1] // LANES
    for m in range(chunks):
        rawf[m * 8 : m * 8 + rows, :] = raw[:, m * LANES : (m + 1) * LANES].astype(jnp.float32)
    rawf[chunks * 8 :, :] = jnp.zeros((rawf.shape[0] - chunks * 8, LANES), jnp.float32)
    tapf[0:1, 0:TAPS] = taps[...]

    wide = REACH * LANES
    tap_rows = jnp.broadcast_to(tapf[0:1, :], (FINE, wide))
    step = DEC * lax.broadcasted_iota(jnp.int32, (FINE, wide), 0)
    for w in range(wins):
        off = offs[w]
        first, rest = off // LANES, off % LANES
        shift = step + rest
        x = tap_rows
        for b in range((LANES + DEC * FINE - 1).bit_length()):
            x = jnp.where((shift >> b) & 1 == 1, pltpu.roll(x, 1 << b, 1), x)
        high = x.astype(jnp.bfloat16)
        low = (x - high.astype(jnp.float32)).astype(jnp.bfloat16)
        toeplitz = jnp.concatenate([high, low], axis=0)
        total = jnp.zeros((2 * FINE, rows * COARSE), jnp.float32)
        for s in range(REACH):
            seen = jnp.concatenate(
                [rawf[pl.ds((first + s) * 8 + r, COARSE, stride=8), :] for r in range(rows)], axis=0
            ).astype(jnp.bfloat16)
            total = total + lax.dot_general(
                toeplitz[:, s * LANES : (s + 1) * LANES], seen, (((1,), (1,)), ((), ())),
                preferred_element_type=jnp.float32)
        deci = (total[:FINE] + total[FINE:]).astype(jnp.bfloat16)
        for r in range(rows):
            part = deci[:, r * COARSE : (r + 1) * COARSE]
            z = jnp.dot(part, forward[:COARSE, :], preferred_element_type=jnp.float32) + jnp.dot(
                part, forward[COARSE:, :], preferred_element_type=jnp.float32)
            at = (w * rows + r) * FINE
            zbuf[0, at : at + FINE, :] = z[:, :LANES]
            zbuf[1, at : at + FINE, :] = z[:, LANES:]
    points = []
    for n in range(FINE):
        y = zbuf[0, pl.ds(n, unit, stride=FINE), :]
        ys = zbuf[1, pl.ds(n, unit, stride=FINE), :]
        c, s = twiddle[0, n : n + 1, :], twiddle[1, n : n + 1, :]
        points.append((c * y + s * ys, c * ys - s * y))
    bins = fft(points)
    mine = (p * 2 + sec) * subs + sub
    for k in range(BANDS):
        x = bins[k][0]
        power = jnp.sum(x * x, axis=1, keepdims=True) * (1.0 / BAND)
        held[mine, :, k * LANES : (k + 1) * LANES] = (x * lax.rsqrt(power + 1e-06)).astype(jnp.bfloat16)

    pl.semaphore_wait(barrier, pairs * subs)

    def send(slot, send_sem, device):
        return pltpu.make_async_remote_copy(
            src_ref=held.at[slot], dst_ref=held.at[slot], send_sem=send_sem,
            recv_sem=recv.at[slot], device_id=device, device_id_type=MESH)

    near = [p]
    for i in range(1, pairs):
        at = jnp.int32(0)
        for q in range(pairs):
            at = jnp.where(p == q, sorted(range(pairs), key=lambda t: (abs(t - q), t))[i], at)
        near.append(at)
    copies = []
    for dp in range(pairs - 1, -1, -1):
        for d in range(subs - 1, -1, -1):
            if not (dp or d):
                continue
            copies.append(send(mine, x_send.at[dp, d], {"pairs": near[dp], "sub": lax.rem(sub + d, subs)}))
            copies[-1].start()
    for dp in range(pairs):
        slot = (near[dp] * 2 + sec) * subs + sub
        if dp:
            send(slot, z_send.at[0], {"section": 1 - sec}).wait_recv()
        copies.append(send(slot, c_send.at[dp, 0], {"section": 1 - sec}))
        copies[-1].start()
    for dp in range(pairs):
        for d in range(1, subs):
            slot = (near[dp] * 2 + sec) * subs + lax.rem(sub + d, subs)
            send(slot, z_send.at[0], {"section": 1 - sec}).wait_recv()
            copies.append(send(slot, c_send.at[dp, d], {"section": 1 - sec}))
            copies[-1].start()

    count = pairs * block
    lead_rows = leads * subs * unit
    depth = pairs * 2 * subs * unit
    col = lax.broadcasted_iota(jnp.int32, (1, depth), 1)
    col_row = (col // (unit * subs)) * rows + col % rows
    plain = lax.broadcasted_iota(jnp.int32, (1, count), 1)
    col_id = jnp.full((1, depth), -1, jnp.int32)
    row_id = jnp.full((1, count), -1, jnp.int32)
    for i in range(count):
        col_id = jnp.where(col_row == i, ids[i], col_id)
        row_id = jnp.where(plain == i, ids[i], row_id)
    line = lax.broadcasted_iota(jnp.int32, (lead_rows, 1), 0)
    own = table[0, p * slots]
    for s in range(1, slots):
        own = jnp.maximum(own, table[0, p * slots + s])
    lead = own * block + (sec * subs + sub) * leads + line // (subs * unit)
    place = (line // rows) % (subs * wins)
    col_place = (col // unit) % subs * wins + (col // rows) % wins
    pick = jnp.where((lead == col_id) & (place == col_place), 1.0, 0.0).astype(jnp.bfloat16)
    entry = lax.broadcasted_iota(jnp.int32, (slots * block, 1), 0)
    want = jnp.full((slots * block, 1), -1, jnp.int32)
    for s in range(slots):
        live = jnp.where(table[0, p * slots + s] >= 0, table[1, p * slots + s] * block, -block)
        want = jnp.where(entry // block == s, live + entry % block, want)
    order = jnp.where(want == row_id, 1.0, 0.0).astype(jnp.bfloat16)

    for dp in range(pairs):
        for d in range(subs):
            slot = (lax.rem(p + dp, pairs) * 2 + 1 - sec) * subs + lax.rem(sub + d, subs)
            send(slot, z_send.at[0], {"section": 1 - sec}).wait_recv()
    for copy in copies:
        copy.wait_send()

    left = lax.broadcasted_iota(jnp.int32, (8, LANES), 1) < BAND
    top = lax.broadcasted_iota(jnp.int32, (8, LANES), 0) < rows
    scale = 1.0 / (wins * subs)
    width = 2 * LANES

    for base in range(0, NF, width):
        every = held[:, :, pl.ds(base, width)].astype(jnp.float32)
        flat = every.reshape(depth, width)
        heads = jnp.dot(pick, flat.astype(jnp.bfloat16), preferred_element_type=jnp.float32)
        crossed = [[[] for _ in range(2)] for _ in range(leads)]
        for h in range(2):
            lanes = slice(h * LANES, (h + 1) * LANES)
            half = heads[:, lanes]
            swap = pltpu.roll(half, BAND, 1)
            for q in range(pairs):
                for a in range(leads):
                    sums = []
                    for source in (half, swap):
                        two = []
                        for c in range(2):
                            t = None
                            for u in range(subs):
                                g = (q * 2 + c) * subs + u
                                at = (a * subs + u) * unit
                                v = flat[g * unit : (g + 1) * unit, lanes] * source[at : at + unit, :]
                                t = v if t is None else t + v
                            two.append(t + pltpu.roll(t, rows, 0))
                        sums.append(jnp.where(top, two[0], two[1]))
                    re, im = sums
                    crossed[a][h].append(
                        jnp.where(left, re + pltpu.roll(re, BAND, 1), pltpu.roll(im, BAND, 1) - im) * scale)
        for a in range(leads):
            cross = jnp.concatenate(
                [jnp.concatenate(crossed[a][h], axis=0) for h in range(2)], axis=1).astype(jnp.bfloat16)
            got = jnp.dot(order, cross, preferred_element_type=jnp.float32)
            lhs[a * slots * block : (a + 1) * slots * block, pl.ds(base, width)] = got.astype(jnp.bfloat16)

    load_inverse.wait()

    for base in range(0, NF, width):
        out[:, pl.ds(base, width)] = jnp.dot(
            lhs[...], inv[:, pl.ds(base, width)], preferred_element_type=jnp.float32)


def solution(mesh):
    pairs, subs = mesh.shape["pairs"], mesh.shape["sub"]

    def body(raw_record, fir_taps, channel_ids, offsets, pair_table):
        rows, wins = raw_record.shape[0], offsets.shape[0]
        slots = pair_table.shape[0] // pairs
        block = 2 * rows
        leads = block // (2 * subs)
        unit = rows * wins
        assert unit == 8 and block == 8 and wins == 2
        chunks = raw_record.shape[1] // LANES
        units = pairs * 2 * subs
        vmem = pl.BlockSpec(memory_space=pltpu.VMEM)
        hbm = pl.BlockSpec(memory_space=pltpu.HBM)
        forward, twiddle, inverse = tables()
        total = leads * slots * block
        result = pl.pallas_call(
            functools.partial(kernel, (pairs, subs, rows, wins, slots, leads)),
            out_shape=jax.ShapeDtypeStruct((total, NF), jnp.float32),
            in_specs=[hbm] * 8,
            out_specs=vmem,
            scratch_shapes=[
                pltpu.VMEM(raw_record.shape, raw_record.dtype),
                pltpu.VMEM((1, TAPS), jnp.float32),
                pltpu.SMEM(channel_ids.shape, jnp.int32),
                pltpu.SMEM(offsets.shape, jnp.int32),
                pltpu.SMEM(pair_table.shape[::-1], jnp.int32),
                pltpu.VMEM(forward.shape, jnp.bfloat16),
                pltpu.VMEM(twiddle.shape, jnp.float32),
                pltpu.SemaphoreType.DMA((7,)),
                pltpu.VMEM((units, unit, NF), jnp.bfloat16),
                pltpu.VMEM(((chunks + 8) * 8, LANES), jnp.float32),
                pltpu.VMEM((8, REACH * LANES), jnp.float32),
                pltpu.VMEM((2, unit * FINE, LANES), jnp.float32),
                pltpu.VMEM((total, NF), jnp.bfloat16),
                pltpu.VMEM((NF, NF), jnp.bfloat16),
                pltpu.SemaphoreType.DMA,
                pltpu.SemaphoreType.DMA((pairs,)),
                pltpu.SemaphoreType.DMA((pairs, subs)),
                pltpu.SemaphoreType.DMA((pairs, subs)),
                pltpu.SemaphoreType.DMA((units,)),
            ],
            compiler_params=pltpu.CompilerParams(
                collective_id=0, has_side_effects=True, vmem_limit_bytes=48*2**20),
        )(*[pltpu.with_memory_space_constraint(v, pltpu.HBM) for v in (raw_record, fir_taps.reshape(1, TAPS), channel_ids, offsets, pair_table.T,
          jnp.asarray(forward), jnp.asarray(twiddle), jnp.asarray(inverse))])
        return result.reshape(leads, slots, block, NF)

    return jax.shard_map(
        body,
        mesh=mesh,
        in_specs=(
            P(("groups", "pairs", "section"), "sub"),
            P(),
            P("groups"),
            P(("groups", "sub")),
            P("groups", None),
        ),
        out_specs=P(("section", "sub"), ("groups", "pairs"), None, None),
        check_vma=False,
    )
```
